32 devices in a mesh: dp: 8 (over z, y), mp: 4 (over x, core).
Axes of the slice: x: 2, y: 2, z: 4, core: 2. Of those that a mesh axis runs over, the one named last changes fastest.
Arguments:
- gradient: float32 [4096, 18432], P(('mp', 'dp')), may hold values from -6 to 6
- momentum: float32 [4096, 18432], P(('mp', 'dp')), may hold values from -6 to 6
- left_basis: float32 [320, 512, 512], P(('mp', 'dp')), may hold values from -0.25 to 0.25
- right_basis: float32 [320, 512, 512], P(('mp', 'dp')), may hold values from -0.25 to 0.25
- second_moment: float32 [320, 512, 512], P(('mp', 'dp')), may hold values from 0.05 to 2
- block_slot: int32 [288], replicated, may hold values from 0 to 319, as said below
Outputs:
- update: float32 [4096, 18432], P(('mp', 'dp'))
- momentum_out: float32 [4096, 18432], P(('mp', 'dp'))
- moment_out: float32 [320, 512, 512], P(('mp', 'dp'))
The draws below stay inside these ranges and needn't reach their ends.
Inputs may be any that keep to these rules, and one draw needn't show every extreme that they name: `block_slot`: all entries differ. A block's slot lies on a device of the same mp index as the devices that hold the block's rows. A device owns at most 9 blocks, a bound that some device reaches, and at most 5 blocks of one row of blocks, a bound that some device reaches.
All inputs are finite; a program needn't handle non-finite values.
Results may differ from the reference program's by a relative error of at most 0.000084.
Values sent between devices are 32-bit elements; how exact they have to be, the bound alone decides.
A program may use at most 192 MiB of HBM per device.

```python
import math
import jax
import jax.numpy as jnp
from jax import lax

ROWS = 4096
COLS = 18432
BLOCK = 512
ROW_BLOCKS = 8
COL_BLOCKS = 36
BLOCKS = 288
SLOTS = 10
N_DP = 8
N_MP = 4
DEVICES = 32


def draw_block_slot(key, part):
    group_rows = ROW_BLOCKS // N_MP
    order_keys = jax.random.split(jax.random.fold_in(key, 11), N_MP)
    device_order = jax.vmap(lambda sub_key: jax.random.permutation(sub_key, N_DP))(order_keys).astype(jnp.int32)
    slot_turn = jax.random.randint(jax.random.fold_in(key, 12), (DEVICES,), 0, SLOTS).astype(jnp.int32)
    row_keys = jax.random.split(jax.random.fold_in(key, 13), ROW_BLOCKS)
    column_place = jax.vmap(lambda sub_key: jax.random.permutation(sub_key, COL_BLOCKS))(row_keys).astype(jnp.int32)
    row_index = jnp.arange(ROW_BLOCKS, dtype=jnp.int32)
    group_ids = row_index // group_rows
    local_rows = row_index % group_rows
    position = local_rows[:, None] * COL_BLOCKS + column_place
    owner_dp = device_order[group_ids[:, None], position % N_DP]
    owner_ids = group_ids[:, None] * N_DP + owner_dp
    slot_ids = (position // N_DP + slot_turn[owner_ids]) % SLOTS
    return (owner_ids * SLOTS + slot_ids).reshape(BLOCKS).astype(jnp.int32)


def block_scale(stream_key, extent, cuts, smallest, largest):
    level = 1.0
    for axis_at, blocks in cuts:
        steps = jax.random.uniform(jax.random.fold_in(jax.random.fold_in(stream_key, 6), axis_at), (blocks,), jnp.float32, smallest / len(cuts), largest / len(cuts))
        level = level * jnp.repeat(jnp.exp(steps), extent[axis_at] // blocks).reshape((-1,) + (1,) * (len(extent) - 1 - axis_at))
    return level


def normal_values(stream_key, dims, scale, reach, shards=(), kind=jnp.bfloat16):
    factor_of = block_scale(stream_key, dims, shards, -0.22, 0.18) if shards else 1.0
    result = jax.random.normal(stream_key, dims, jnp.float32) * scale * factor_of
    return jnp.minimum(jnp.maximum(result, -reach), reach).astype(kind)


def setup_inputs(seed: int = 0) -> dict:
    key_list = jax.random.split(jax.random.key(seed), 7)
    gradient = normal_values(key_list[0], (ROWS, COLS), 1.0, 6.0, ((0, 32),), jnp.float32)
    momentum = normal_values(key_list[1], (ROWS, COLS), 1.0, 6.0, ((0, 32),), jnp.float32)
    left_basis = normal_values(key_list[2], (DEVICES * SLOTS, BLOCK, BLOCK), BLOCK ** -0.5, 0.25, ((0, 32),), jnp.float32)
    right_basis = normal_values(key_list[3], (DEVICES * SLOTS, BLOCK, BLOCK), BLOCK ** -0.5, 0.25, ((0, 32),), jnp.float32)
    second_moment = jnp.clip(jnp.exp(math.log(2.0) - 3.6888794 * jax.random.uniform(key_list[4], (DEVICES * SLOTS, BLOCK, BLOCK), jnp.float32) ** block_scale(key_list[4], (DEVICES * SLOTS, BLOCK, BLOCK), ((0, 32),), -0.2, 0.2)), 0.05, 2.0)
    block_slot = draw_block_slot(jax.random.fold_in(key_list[6], 71), 0)
    return {"gradient": gradient, "momentum": momentum, "left_basis": left_basis, "right_basis": right_basis, "second_moment": second_moment, "block_slot": block_slot}


BETA_ONE = 0.9
BETA_TWO = 0.95
EPSILON = 1e-08
PRECISE = lax.Precision.HIGHEST

def to_blocks(matrix):
    shaped = matrix.reshape(ROWS // BLOCK, BLOCK, COLS // BLOCK, BLOCK)
    return shaped.transpose(0, 2, 1, 3).reshape(BLOCKS, BLOCK, BLOCK)

def from_blocks(blocked):
    shaped = blocked.reshape(ROWS // BLOCK, COLS // BLOCK, BLOCK, BLOCK)
    return shaped.transpose(0, 2, 1, 3).reshape(ROWS, COLS)

def reference(gradient, momentum, left_basis, right_basis, second_moment, block_slot):
    momentum_out = BETA_ONE * momentum + (1.0 - BETA_ONE) * gradient
    grad_blocks = to_blocks(gradient)
    mom_blocks = to_blocks(momentum_out)

    def one_block(operands):
        grad_block, mom_block, slot_index = operands
        basis_left = left_basis[slot_index]
        basis_right = right_basis[slot_index]
        grad_rot = jnp.dot(jnp.dot(basis_left.T, grad_block, precision=PRECISE), basis_right, precision=PRECISE)
        mom_rot = jnp.dot(jnp.dot(basis_left.T, mom_block, precision=PRECISE), basis_right, precision=PRECISE)
        moment_new = BETA_TWO * second_moment[slot_index] + (1.0 - BETA_TWO) * grad_rot * grad_rot
        step_rot = mom_rot / (jnp.sqrt(moment_new) + EPSILON)
        step_block = jnp.dot(jnp.dot(basis_left, step_rot, precision=PRECISE), basis_right.T, precision=PRECISE)
        return (step_block, moment_new)
    step_blocks, moment_blocks = lax.map(one_block, (grad_blocks, mom_blocks, block_slot))
    update = from_blocks(step_blocks)
    moment_out = second_moment.at[block_slot].set(moment_blocks)
    return (update, momentum_out, moment_out)
```

```python
import functools
import itertools

import jax
import jax.numpy as jnp
import numpy as np
from jax import lax
from jax.experimental import pallas as pl
from jax.experimental.pallas import tpu as pltpu
from jax.sharding import PartitionSpec as P

BETA_ONE = 0.9
BETA_TWO = 0.95
EPSILON = 1e-08
F32 = jnp.float32
BF16 = jnp.bfloat16
NN = (((1,), (0,)), ((), ()))
NT = (((1,), (1,)), ((), ()))
VMEM_LIMIT = 66_900_000
AHEAD = 2
ANY = pl.BlockSpec(memory_space=pl.ANY)
SMEM = pl.BlockSpec(memory_space=pltpu.SMEM)


def split(x):
    hi = x.astype(BF16)
    return hi, (x - hi.astype(F32)).astype(BF16)


def product(ah, al, bh, bl, dims=NN):
    dot = functools.partial(lax.dot_general, dimension_numbers=dims, preferred_element_type=F32)
    return dot(ah, bh) + (dot(ah, bl) + dot(al, bh))


def pack_kernel(cols, block, place_ref, grad_ref, mom_ref, packed_ref, new_ref, grad, mom, new, in_sem, out_sem):
    col_blocks = place_ref.shape[0]
    width = cols * block

    def fetch(i):
        at = pl.ds(i * width, width)
        return (
            pltpu.make_async_copy(grad_ref.at[:, at], grad.at[:, at], in_sem.at[i, 0]),
            pltpu.make_async_copy(mom_ref.at[:, at], mom.at[:, at], in_sem.at[i, 1]),
        )

    def put(i):
        at = pl.ds(i * width, width)
        copies = [pltpu.make_async_copy(new.at[:, at], new_ref.at[:, at], out_sem.at[i, 2 * cols])]
        for j in range(cols):
            part = pl.ds(i * width + j * block, block)
            spot = place_ref[i * cols + j]
            copies.append(pltpu.make_async_copy(grad.at[:, part], packed_ref.at[spot, 0], out_sem.at[i, 2 * j]))
            copies.append(pltpu.make_async_copy(new.at[:, part], packed_ref.at[spot, 1], out_sem.at[i, 2 * j + 1]))
        return copies

    steps = col_blocks // cols
    for i in range(steps):
        for copy in fetch(i):
            copy.start()
    for i in range(steps):
        for copy in fetch(i):
            copy.wait()
        at = pl.ds(i * width, width)
        new[:, at] = BETA_ONE * mom[:, at] + (1.0 - BETA_ONE) * grad[:, at]
        for copy in put(i):
            copy.start()
    for i in range(steps):
        for copy in put(i):
            copy.wait()


def place_kernel(block, place_ref, rank_ref, live_ref, got_ref, rank_moment_ref, second_ref, update_ref, moment_ref,
                 update, moment, up_sem, mo_sem, out_sem):
    col_blocks = place_ref.shape[0]
    slots = live_ref.shape[0]

    def take(c):
        return pltpu.make_async_copy(got_ref.at[place_ref[c]], update.at[:, pl.ds(c * block, block)], up_sem.at[c])

    for c in range(col_blocks):
        take(c).start()
    for s in range(slots):
        @pl.when(live_ref[s] > 0)
        def _():
            pltpu.make_async_copy(rank_moment_ref.at[rank_ref[s]], moment.at[s], mo_sem.at[s]).start()

        @pl.when(live_ref[s] == 0)
        def _():
            pltpu.make_async_copy(second_ref.at[s], moment.at[s], mo_sem.at[s]).start()

    outs = []
    for c in range(col_blocks):
        take(c).wait()
        at = pl.ds(c * block, block)
        outs.append(pltpu.make_async_copy(update.at[:, at], update_ref.at[:, at], out_sem.at[c]))
        outs[-1].start()
    for s in range(slots):
        pltpu.make_async_copy(second_ref.at[s], moment.at[s], mo_sem.at[s]).wait()
        outs.append(pltpu.make_async_copy(moment.at[s], moment_ref.at[s], out_sem.at[col_blocks + s]))
        outs[-1].start()
    for copy in outs:
        copy.wait()


def step_kernel(n, ranks, row_sets, group, slot_ref, packed_ref, left_ref, right_ref, second_ref, got_ref, rank_moment_ref,
                recv, left, right, second, lh, ll, th, tl, rh, rl, xh, xl, sh, sl, fresh,
                state_sem, send_sem, recv_sem, back_sem, got_sem, fresh_sem):
    me = lax.axis_index("dp")
    my_set = me // group
    my_part = me % group
    rows = packed_ref.shape[2]
    block = packed_ref.shape[3]
    count = ranks * row_sets
    half = block // 2

    states = (
        pltpu.make_async_copy(left_ref, left, state_sem.at[0]),
        pltpu.make_async_copy(right_ref, right, state_sem.at[1]),
        pltpu.make_async_copy(second_ref, second, state_sem.at[2]),
    )
    for copy in states:
        copy.start()

    barrier = pltpu.get_barrier_semaphore()

    @pl.loop(1, n)
    def _(o):
        pl.semaphore_signal(barrier, inc=1, device_id={"dp": lax.rem(me + o, n)}, device_id_type=pl.DeviceIdType.MESH)

    pl.semaphore_wait(barrier, n - 1)

    def send(r, to):
        k = r * row_sets + my_set
        return pltpu.make_async_remote_copy(
            src_ref=packed_ref.at[to * ranks + r],
            dst_ref=recv.at[k, :, pl.ds(my_part * rows, rows), :],
            send_sem=send_sem.at[to, r],
            recv_sem=recv_sem.at[k, my_part],
            device_id={"dp": to},
            device_id_type=pl.DeviceIdType.MESH,
        )

    def arrived(k, p):
        part = recv.at[k, :, pl.ds(p * rows, rows), :]
        return pltpu.make_async_copy(part, part, recv_sem.at[k, p])

    def give_back(k, p):
        r = k // row_sets
        to = lax.rem(k, row_sets) * group + p
        return to, pltpu.make_async_remote_copy(
            src_ref=recv.at[k, 0, pl.ds(p * rows, rows), :],
            dst_ref=got_ref.at[me * ranks + r],
            send_sem=back_sem.at[k, p],
            recv_sem=got_sem.at[me * ranks + r],
            device_id={"dp": to},
            device_id_type=pl.DeviceIdType.MESH,
        )

    @pl.loop(0, ranks)
    def _(r):
        k = r * row_sets + my_set
        pltpu.make_async_copy(
            packed_ref.at[me * ranks + r],
            recv.at[k, :, pl.ds(my_part * rows, rows), :],
            recv_sem.at[k, my_part],
        ).start()

        @pl.loop(1, n)
        def _(o):
            send(r, lax.rem(me + o, n)).start()

    for copy in states:
        copy.wait()

    @pl.loop(0, count)
    def _(k):
        slot = slot_ref[k]
        spot = lax.rem(k, 2)

        @pl.loop(0, block // 128)
        def _(i):
            at = pl.ds(i * 128, 128)
            piece = left[slot, at, :]
            lh[at, :], ll[at, :] = split(piece)
            th[:, at], tl[:, at] = split(piece.T)
            rh[at, :], rl[at, :] = split(right[slot, at, :])

        @pl.loop(0, group)
        def _(p):
            arrived(k, p).wait()

        @pl.when(k >= 2)
        def _():
            pltpu.make_async_copy(fresh.at[spot], rank_moment_ref.at[k - 2], fresh_sem.at[spot]).wait()

        @pl.loop(0, block // 128)
        def _(i):
            at = pl.ds(i * 128, 128)
            for x in range(2):
                xh[x, at, :], xl[x, at, :] = split(recv[k, x, at, :])

        @pl.loop(0, 2)
        def _(i):
            at = pl.ds(i * half, half)

            def rotate(x):
                partial = product(th[at, :], tl[at, :], xh[x], xl[x])
                ph, plow = split(partial)
                return product(ph, plow, rh[...], rl[...])

            grad_rot = rotate(0)
            moment = BETA_TWO * second[slot, at, :] + (1.0 - BETA_TWO) * grad_rot * grad_rot
            fresh[spot, at, :] = moment
            step = rotate(1) / (jnp.sqrt(moment) + EPSILON)
            sh[at, :], sl[at, :] = split(step)

        pltpu.make_async_copy(fresh.at[spot], rank_moment_ref.at[k], fresh_sem.at[spot]).start()

        @pl.loop(0, 2)
        def _(i):
            at = pl.ds(i * half, half)
            partial = product(lh[at, :], ll[at, :], sh[...], sl[...])
            ph, plow = split(partial)
            recv[k, 0, at, :] = product(ph, plow, rh[...], rl[...], NT)

        @pl.loop(0, group)
        def _(p):
            to, copy = give_back(k, p)

            @pl.when(to != me)
            def _():
                copy.start()

            @pl.when(to == me)
            def _():
                pltpu.make_async_copy(
                    recv.at[k, 0, pl.ds(p * rows, rows), :],
                    got_ref.at[me * ranks + k // row_sets],
                    got_sem.at[me * ranks + k // row_sets],
                ).start()

    for k in range(max(count - 2, 0), count):
        pltpu.make_async_copy(fresh.at[k % 2], rank_moment_ref.at[k], fresh_sem.at[k % 2]).wait()

    @pl.loop(0, ranks)
    def _(r):
        @pl.loop(1, n)
        def _(o):
            send(r, lax.rem(me + o, n)).wait_send()

    @pl.loop(0, count)
    def _(k):
        @pl.loop(0, group)
        def _(p):
            to, copy = give_back(k, p)

            @pl.when(to != me)
            def _():
                copy.wait_send()

    @pl.loop(0, n * ranks)
    def _(q):
        pltpu.make_async_copy(got_ref.at[q], got_ref.at[q], got_sem.at[q]).wait()


def head_kernel(layout, ahead, slots_ref, plan_ref, grad_ref, mom_ref, early_ref, choice_ref, grad, mom, new, in_sem, out_sem):
    n, group, slots, ranks, block = layout
    me = lax.axis_index("dp")
    at_mp = lax.axis_index("mp")
    shape = slots_ref.shape
    row = lax.broadcasted_iota(jnp.int32, shape, 0)
    col = lax.broadcasted_iota(jnp.int32, shape, 1)
    line = lax.broadcasted_iota(jnp.int32, (shape[0], 1), 0)
    local = slots_ref[...] - (row // 2) * (n * slots)
    low = lax.rem(me + group, n) * slots
    wanted = (row == at_mp * 2 + me // group) & (local >= low) & (local < low + slots)
    column = []
    for r in range(ahead):
        at = jnp.min(jnp.where(wanted, col, shape[1] - 1))
        wanted = wanted & (col > at)
        column.append(at)

    def fetch(r):
        at = pl.ds(pl.multiple_of(column[r] * block, block), block)
        return (
            pltpu.make_async_copy(grad_ref.at[:, at], grad.at[r], in_sem.at[r, 0]),
            pltpu.make_async_copy(mom_ref.at[:, at], mom.at[r], in_sem.at[r, 1]),
        )

    def put(r):
        return (
            pltpu.make_async_copy(grad.at[r], early_ref.at[r, 0], out_sem.at[r, 0]),
            pltpu.make_async_copy(new.at[r], early_ref.at[r, 1], out_sem.at[r, 1]),
        )

    for r in range(ahead):
        for copy in fetch(r):
            copy.start()
    total = jnp.zeros((shape[0], 1), jnp.int32)
    for j in range(group):
        low = ((1 - row % 2) * group + j) * slots
        hit = (local >= low) & (local < low + slots)
        total += (jnp.sum(hit.astype(jnp.int32), axis=1, keepdims=True) == ranks).astype(jnp.int32)
    weight = jnp.zeros_like(line)
    for m in range(shape[0] // 2):
        weight = jnp.where(line == 2 * m, (group + 1) ** m, weight)
    choice_ref[0] = plan_ref[jnp.sum(total * weight)]
    for r in range(ahead):
        for copy in fetch(r):
            copy.wait()
        new[r] = BETA_ONE * mom[r] + (1.0 - BETA_ONE) * grad[r]
        for copy in put(r):
            copy.start()
    for r in range(ahead):
        for copy in put(r):
            copy.wait()


def table_layout(n, group, slots, ranks, col_blocks):
    sizes = {
        "slot": 2 * ranks - 1, "source": group, "seat": group, "column": group,
        "place": col_blocks, "rank": slots, "live": slots,
    }
    offsets, at = {}, 0
    for name, size in sizes.items():
        offsets[name] = at
        at += size
    return offsets, at


def fill_table(layout, slots_ref, table, owned, fifth):
    n, group, slots, ranks, block = layout
    col_blocks = slots_ref.shape[0] // (2 * lax.axis_size("mp"))
    at, size = table_layout(n, group, slots, ranks, col_blocks)
    me = lax.axis_index("dp")
    at_mp = lax.axis_index("mp")
    my_set = me // group
    base = ranks - 1
    turn = -(-base // 2)

    @pl.loop(0, size)
    def _(i):
        table[i] = 0

    @pl.loop(0, 2 * n)
    def _(i):
        owned[i] = 0
        fifth[i] = -1

    for row_set in range(2):
        @pl.loop(0, col_blocks)
        def _(c):
            seat = slots_ref[(at_mp * 2 + row_set) * col_blocks + c] - at_mp * (n * slots)
            owner = lax.div(seat, slots)
            local = seat - owner * slots
            rank = owned[row_set * n + owner]
            owned[row_set * n + owner] = rank + 1
            k = jnp.where(rank < base, 2 * rank + row_set + lax.div(rank, turn), 2 * turn)

            @pl.when(owner == me)
            def _():
                table[at["slot"] + k] = local
                table[at["rank"] + local] = k
                table[at["live"] + local] = 1

            @pl.when(rank == base)
            def _():
                fifth[row_set * n + owner] = c

            @pl.when(my_set == row_set)
            def _():
                table[at["place"] + c] = owner * base + rank

    here, there = my_set * group, (1 - my_set) * group
    out, back = jnp.int32(0), jnp.int32(0)
    for j in range(group):
        kept = fifth[my_set * n + here + j]

        @pl.when(kept >= 0)
        def _():
            table[at["place"] + kept] = n * base + j

        sent = fifth[my_set * n + there + j]
        table[at["column"] + j] = -1

        @pl.when(sent >= 0)
        def _():
            table[at["place"] + sent] = n * base + group + out

        guest = fifth[(1 - my_set) * n + here + j]
        table[at["source"] + j] = jnp.where(guest >= 0, back, -1)

        @pl.when(guest >= 0)
        def _():
            table[at["seat"] + back] = j

        @pl.when(sent >= 0)
        def _():
            table[at["column"] + out] = sent

        out += (sent >= 0).astype(jnp.int32)
        back += (guest >= 0).astype(jnp.int32)


def lead_kernel(cols, layout, slots_ref, grad_ref, mom_ref, packed_ref, new_ref, table, *refs):
    n, group, slots, ranks, block = layout
    lanes, (grad, mom, new, owned, fifth, in_sem, out_sem, lane_sem) = refs[:group], refs[group:]
    width = cols * block
    steps = grad_ref.shape[1] // width
    at, _ = table_layout(n, group, slots, ranks, steps * cols)

    def fetch(i):
        part = pl.ds(i * width, width)
        return (
            pltpu.make_async_copy(grad_ref.at[:, part], grad.at[:, part], in_sem.at[i, 0]),
            pltpu.make_async_copy(mom_ref.at[:, part], mom.at[:, part], in_sem.at[i, 1]),
        )

    def put(i):
        part = pl.ds(i * width, width)
        copies = [pltpu.make_async_copy(new.at[:, part], new_ref.at[:, part], out_sem.at[i, 2 * cols])]
        for j in range(cols):
            part = pl.ds(i * width + j * block, block)
            spot = table[at["place"] + i * cols + j]
            copies.append(pltpu.make_async_copy(grad.at[:, part], packed_ref.at[spot, 0], out_sem.at[i, 2 * j]))
            copies.append(pltpu.make_async_copy(new.at[:, part], packed_ref.at[spot, 1], out_sem.at[i, 2 * j + 1]))
        return copies

    def lane(i):
        part = pl.ds(pl.multiple_of(jnp.maximum(table[at["column"] + i], 0) * block, block), block)
        return (
            pltpu.make_async_copy(grad.at[:, part], lanes[i].at[0], lane_sem.at[i, 0]),
            pltpu.make_async_copy(new.at[:, part], lanes[i].at[1], lane_sem.at[i, 1]),
        )

    for i in range(steps):
        for copy in fetch(i):
            copy.start()
    fill_table(layout, slots_ref, table, owned, fifth)
    for i in range(steps):
        for copy in fetch(i):
            copy.wait()
        part = pl.ds(i * width, width)
        new[:, part] = BETA_ONE * mom[:, part] + (1.0 - BETA_ONE) * grad[:, part]
        for copy in put(i):
            copy.start()
    for i in range(group):
        for copy in lane(i):
            copy.start()
    for i in range(steps):
        for copy in put(i):
            copy.wait()
    for i in range(group):
        for copy in lane(i):
            copy.wait()


def lane_kernel(layout, place_at, table, packed_ref, left_ref, right_ref, second_ref, early_ref, *refs):
    n, group, slots, ranks, block = layout
    guests, got_ref, rank_moment_ref = refs[:group], refs[group], refs[group + 1]
    backs, refs = refs[group + 2:2 * group + 2], refs[2 * group + 2:]
    (recv, left, right, second, lh, ll, th, tl, rh, rl, xh, xl, sh, sl, fresh, lane, stage, extra,
     state_sem, send_sem, recv_sem, back_sem, got_sem, fresh_sem, lane_sem, stage_sem, extra_sem, return_sem, keep_sem) = refs
    me = lax.axis_index("dp")
    my_set = me // group
    my_part = me % group
    partner = lax.rem(me + group, n)
    ahead = early_ref.shape[0]
    rows = packed_ref.shape[2]
    base = ranks - 1
    turn = -(-base // 2)
    last = 2 * turn
    count = 2 * base + 1
    half = block // 2
    MESH = pl.DeviceIdType.MESH

    states = (
        pltpu.make_async_copy(left_ref, left, state_sem.at[0]),
        pltpu.make_async_copy(right_ref, right, state_sem.at[1]),
        pltpu.make_async_copy(second_ref, second, state_sem.at[2]),
    )
    own = pltpu.make_async_copy(packed_ref.at[pl.ds(n * base, group)], stage, state_sem.at[3])
    own.start()
    for i in range(group):
        pltpu.make_async_copy(guests[i], lane.at[i], lane_sem.at[i]).start()
    for copy in states:
        copy.start()

    barrier = pltpu.get_barrier_semaphore()

    @pl.loop(1, n)
    def _(o):
        pl.semaphore_signal(barrier, inc=1, device_id={"dp": lax.rem(me + o, n)}, device_id_type=MESH)

    pl.semaphore_wait(barrier, n - 1)

    def enter(i):
        return pltpu.make_async_copy(guests[i], lane.at[i], lane_sem.at[i])

    def send(r, to):
        k = 2 * r + my_set + r // turn
        return pltpu.make_async_remote_copy(
            src_ref=packed_ref.at[to * base + r],
            dst_ref=recv.at[k, :, pl.ds(my_part * rows, rows), :],
            send_sem=send_sem.at[to, r],
            recv_sem=recv_sem.at[k, my_part],
            device_id={"dp": to},
            device_id_type=MESH,
        )

    def pass_on(j):
        return pltpu.make_async_remote_copy(
            src_ref=stage.at[j],
            dst_ref=recv.at[last, :, pl.ds(my_part * rows, rows), :],
            send_sem=stage_sem.at[j],
            recv_sem=recv_sem.at[last, my_part],
            device_id={"dp": my_set * group + j},
            device_id_type=MESH,
        )

    def arrived(k, p):
        part = recv.at[k, :, pl.ds(p * rows, rows), :]
        return pltpu.make_async_copy(part, part, recv_sem.at[k, p])

    def give_back(k, p):
        dense = k - k // (last + 1)
        to = lax.rem(dense, 2) * group + p
        spot = me * base + dense // 2
        return to, spot, pltpu.make_async_remote_copy(
            src_ref=recv.at[k, 0, pl.ds(p * rows, rows), :],
            dst_ref=got_ref.at[spot],
            send_sem=back_sem.at[k, p],
            recv_sem=got_sem.at[spot],
            device_id={"dp": to},
            device_id_type=MESH,
        )

    def give_extra(p):
        return pltpu.make_async_remote_copy(
            src_ref=recv.at[last, 0, pl.ds(p * rows, rows), :],
            dst_ref=extra.at[my_part],
            send_sem=back_sem.at[last, p],
            recv_sem=extra_sem.at[my_part],
            device_id={"dp": my_set * group + p},
            device_id_type=MESH,
        )

    def leave(i):
        return pltpu.make_async_copy(recv.at[last, 1, pl.ds(i * rows, rows), :], backs[i], return_sem.at[i])

    def keep(j):
        return pltpu.make_async_copy(extra.at[j], got_ref.at[n * base + j], keep_sem.at[j])

    def spread(first, end):
        @pl.loop(first, end)
        def _(r):
            k = 2 * r + my_set + r // turn
            pltpu.make_async_copy(
                packed_ref.at[me * base + r],
                recv.at[k, :, pl.ds(my_part * rows, rows), :],
                recv_sem.at[k, my_part],
            ).start()

            @pl.loop(1, n)
            def _(o):
                to = lax.rem(me + o, n)

                @pl.when((to != partner) | (r >= ahead))
                def _():
                    send(r, to).start()

    for r in range(ahead):
        k = 2 * r + 1 - my_set + r // turn
        pltpu.make_async_copy(
            early_ref.at[r], recv.at[k, :, pl.ds(my_part * rows, rows), :], recv_sem.at[k, my_part]
        ).start()
    spread(0, turn)
    own.wait()
    for i in range(group):
        enter(i).wait()

    @pl.loop(0, group)
    def _(j):
        source = table[place_at["source"] + j]
        fetched = jnp.maximum(source, 0)
        for x in range(2):
            stage[j, x] = jnp.where(source >= 0, lane[fetched, x], stage[j, x])

    @pl.loop(0, group)
    def _(j):
        @pl.when(j != my_part)
        def _():
            pass_on(j).start()

        @pl.when(j == my_part)
        def _():
            pltpu.make_async_copy(
                stage.at[j], recv.at[last, :, pl.ds(my_part * rows, rows), :], recv_sem.at[last, my_part]
            ).start()

    spread(turn, base)
    for copy in states:
        copy.wait()

    @pl.loop(0, count)
    def _(k):
        slot = table[place_at["slot"] + k]

        @pl.when(k == last + 2)
        def _():
            for j in range(group):
                pltpu.make_async_copy(extra.at[j], extra.at[j], extra_sem.at[j]).wait()

            for j in range(group):
                recv[last, 1, pl.ds(j * rows, rows), :] = extra[table[place_at["seat"] + j]]

            for j in range(group):
                leave(j).start()
                keep(j).start()

        @pl.loop(0, block // 128)
        def _(i):
            at = pl.ds(i * 128, 128)
            piece = left[slot, at, :]
            lh[at, :], ll[at, :] = split(piece)
            th[:, at], tl[:, at] = split(piece.T)
            rh[at, :], rl[at, :] = split(right[slot, at, :])

        @pl.loop(0, group)
        def _(p):
            arrived(k, p).wait()

        @pl.when(k >= 1)
        def _():
            pltpu.make_async_copy(fresh, rank_moment_ref.at[k - 1], fresh_sem.at[0]).wait()

        @pl.loop(0, block // 128)
        def _(i):
            at = pl.ds(i * 128, 128)
            for x in range(2):
                xh[x, at, :], xl[x, at, :] = split(recv[k, x, at, :])

        @pl.loop(0, 2)
        def _(i):
            at = pl.ds(i * half, half)

            def rotate(x):
                partial = product(th[at, :], tl[at, :], xh[x], xl[x])
                ph, plow = split(partial)
                return product(ph, plow, rh[...], rl[...])

            grad_rot = rotate(0)
            moment = BETA_TWO * second[slot, at, :] + (1.0 - BETA_TWO) * grad_rot * grad_rot
            fresh[at, :] = moment
            step = rotate(1) / (jnp.sqrt(moment) + EPSILON)
            sh[at, :], sl[at, :] = split(step)

        pltpu.make_async_copy(fresh, rank_moment_ref.at[k], fresh_sem.at[0]).start()

        @pl.loop(0, 2)
        def _(i):
            at = pl.ds(i * half, half)
            partial = product(lh[at, :], ll[at, :], sh[...], sl[...])
            ph, plow = split(partial)
            recv[k, 0, at, :] = product(ph, plow, rh[...], rl[...], NT)

        @pl.loop(0, group)
        def _(p):
            @pl.when(k != last)
            def _():
                to, spot, copy = give_back(k, p)

                @pl.when(to != me)
                def _():
                    copy.start()

                @pl.when(to == me)
                def _():
                    pltpu.make_async_copy(
                        recv.at[k, 0, pl.ds(p * rows, rows), :], got_ref.at[spot], got_sem.at[spot]
                    ).start()

            @pl.when(k == last)
            def _():
                @pl.when(p != my_part)
                def _():
                    give_extra(p).start()

                @pl.when(p == my_part)
                def _():
                    pltpu.make_async_copy(
                        recv.at[last, 0, pl.ds(p * rows, rows), :], extra.at[my_part], extra_sem.at[my_part]
                    ).start()

    pltpu.make_async_copy(fresh, rank_moment_ref.at[count - 1], fresh_sem.at[0]).wait()

    @pl.loop(0, base)
    def _(r):
        @pl.loop(1, n)
        def _(o):
            to = lax.rem(me + o, n)

            @pl.when((to != partner) | (r >= ahead))
            def _():
                send(r, to).wait_send()

    for j in range(group):
        keep(j).wait()
        leave(j).wait()

    @pl.loop(0, group)
    def _(j):
        @pl.when(j != my_part)
        def _():
            pass_on(j).wait_send()
            give_extra(j).wait_send()

    @pl.loop(0, count)
    def _(k):
        @pl.loop(0, group)
        def _(p):
            @pl.when(k != last)
            def _():
                to, spot, copy = give_back(k, p)

                @pl.when(to != me)
                def _():
                    copy.wait_send()

    @pl.loop(0, n * base)
    def _(q):
        pltpu.make_async_copy(got_ref.at[q], got_ref.at[q], got_sem.at[q]).wait()


def settle_kernel(layout, table, got_ref, rank_moment_ref, second_ref, update_ref, moment_ref,
                  update, moment, up_sem, mo_sem, out_sem):
    n, group, slots, ranks, block = layout
    col_blocks = update.shape[1] // block
    at, _ = table_layout(n, group, slots, ranks, col_blocks)
    bound = got_ref.shape[0] - 1

    def take(c):
        spot = jnp.minimum(table[at["place"] + c], bound)
        return pltpu.make_async_copy(got_ref.at[spot], update.at[:, pl.ds(c * block, block)], up_sem.at[c])

    for c in range(col_blocks):
        take(c).start()
    for s in range(slots):
        @pl.when(table[at["live"] + s] > 0)
        def _():
            pltpu.make_async_copy(rank_moment_ref.at[table[at["rank"] + s]], moment.at[s], mo_sem.at[s]).start()

        @pl.when(table[at["live"] + s] == 0)
        def _():
            pltpu.make_async_copy(second_ref.at[s], moment.at[s], mo_sem.at[s]).start()

    outs = []
    for c in range(col_blocks):
        take(c).wait()
        part = pl.ds(c * block, block)
        outs.append(pltpu.make_async_copy(update.at[:, part], update_ref.at[:, part], out_sem.at[c]))
        outs[-1].start()
    for s in range(slots):
        pltpu.make_async_copy(second_ref.at[s], moment.at[s], mo_sem.at[s]).wait()
        outs.append(pltpu.make_async_copy(moment.at[s], moment_ref.at[s], out_sem.at[col_blocks + s]))
        outs[-1].start()
    for copy in outs:
        copy.wait()


def close_kernel(layout, place_at, table, *refs):
    n, group, slots, ranks, block = layout
    guests, (_, update_ref, held, in_sem, out_sem) = refs[:group], refs[group:]

    def take(i):
        return pltpu.make_async_copy(guests[i], held.at[i], in_sem.at[i])

    def put(i):
        spot = pl.multiple_of(jnp.maximum(table[place_at["column"] + i], 0) * block, block)
        return pltpu.make_async_copy(held.at[i], update_ref.at[:, pl.ds(spot, block)], out_sem.at[i])

    def each(act):
        for i in range(group):
            @pl.when(table[place_at["column"] + i] >= 0)
            def _():
                act(i)

    def turn_over(i):
        take(i).wait()
        put(i).start()

    each(lambda i: take(i).start())
    each(turn_over)
    each(lambda i: put(i).wait())


def plans(n_mp, group):
    middle = group // 2
    pairs = [[(c, d) for c in range(1, group + 1) for d in range(1, group + 1) if c + d == s] for s in range(2, 2 * group + 1)]
    wide = group + middle
    keep = [p for p in pairs if group - 1 <= sum(p[0]) <= wide or sum(p[0]) == 2 * group]
    found = []
    for p in keep:
        if sum(p[0]) == group + 1:
            p = [q for q in p if max(q) < group]
        for combo in itertools.product(p, repeat=n_mp // 2):
            found.append(sum(combo, ()))
    choice = np.zeros((group + 1) ** n_mp, np.int32)
    for code in range(choice.size):
        need = [code // (group + 1) ** m % (group + 1) for m in range(n_mp)]
        choice[code] = next(i for i, caps in enumerate(found) if all(c >= q for c, q in zip(caps, need)))
    return found, choice


def paired_step(gradient, momentum, left_basis, right_basis, second_moment, block_slot, ranks, group):
    n = lax.axis_size("dp")
    n_mp = lax.axis_size("mp")
    rows, width = gradient.shape
    slots, block, _ = left_basis.shape
    col_blocks = width // block
    base = ranks - 1
    count = 2 * base + 1
    layout = (n, group, slots, ranks, block)
    place_at, size = table_layout(n, group, slots, ranks, col_blocks)
    found, choice = plans(n_mp, group)
    piece = jax.ShapeDtypeStruct((2, rows, block), F32)
    small = jax.ShapeDtypeStruct((rows, block), F32)
    axes = ("dp", "mp")
    VMEM = pl.BlockSpec(memory_space=pltpu.VMEM)

    early, picked = pl.pallas_call(
        functools.partial(head_kernel, layout, AHEAD),
        out_shape=(jax.ShapeDtypeStruct((AHEAD, 2, rows, block), F32), jax.ShapeDtypeStruct((1,), jnp.int32)),
        in_specs=[VMEM, SMEM, ANY, ANY],
        out_specs=(ANY, SMEM),
        scratch_shapes=[
            pltpu.VMEM((AHEAD, rows, block), F32),
            pltpu.VMEM((AHEAD, rows, block), F32),
            pltpu.VMEM((AHEAD, rows, block), F32),
            pltpu.SemaphoreType.DMA((AHEAD, 2)),
            pltpu.SemaphoreType.DMA((AHEAD, 2)),
        ],
        compiler_params=pltpu.CompilerParams(vmem_limit_bytes=VMEM_LIMIT),
        name="head",
    )(block_slot.reshape(n_mp * 2, col_blocks), jnp.asarray(choice), gradient, momentum)
    branch = picked[0]
    early = lax.ppermute(early, axes, [(d * n_mp + m, (d + group) % n * n_mp + m) for d in range(n) for m in range(n_mp)])

    cols = max(c for c in (1, 2, 3, 4, 6) if col_blocks % c == 0)
    packed, momentum_out, table, *lanes = pl.pallas_call(
        functools.partial(lead_kernel, cols, layout),
        out_shape=(
            jax.ShapeDtypeStruct((n * base + 2 * group, 2, rows, block), F32),
            jax.ShapeDtypeStruct((rows, width), F32),
            jax.ShapeDtypeStruct((size,), jnp.int32),
        ) + (piece,) * group,
        in_specs=[SMEM, ANY, ANY],
        out_specs=(ANY, ANY, SMEM) + (ANY,) * group,
        scratch_shapes=[
            pltpu.VMEM((rows, width), F32),
            pltpu.VMEM((rows, width), F32),
            pltpu.VMEM((rows, width), F32),
            pltpu.SMEM((2 * n,), jnp.int32),
            pltpu.SMEM((2 * n,), jnp.int32),
            pltpu.SemaphoreType.DMA((col_blocks // cols, 2)),
            pltpu.SemaphoreType.DMA((col_blocks // cols, 2 * cols + 1)),
            pltpu.SemaphoreType.DMA((group, 2)),
        ],
        compiler_params=pltpu.CompilerParams(vmem_limit_bytes=VMEM_LIMIT),
        cost_estimate=pl.CostEstimate(flops=3 * rows * width, bytes_accessed=20 * rows * width, transcendentals=0),
        name="lead",
    )(block_slot, gradient, momentum)

    def exchange(caps, values):
        arrived = []
        for i, value in enumerate(values):
            pairs = [(d * n_mp + m, (d + group) % n * n_mp + m) for d in range(n) for m in range(n_mp) if caps[m] > i]
            arrived.append(lax.ppermute(value, axes, pairs) if pairs else jnp.zeros_like(value))
        return arrived

    arrived = lax.switch(branch, [functools.partial(exchange, caps) for caps in found], lanes)

    half_type = pltpu.VMEM((block, block), BF16)
    got, rank_moment, *backs = pl.pallas_call(
        functools.partial(lane_kernel, layout, place_at),
        out_shape=(
            jax.ShapeDtypeStruct((n * base + group, rows, block), F32),
            jax.ShapeDtypeStruct((count, block, block), F32),
        ) + (small,) * group,
        in_specs=[SMEM] + [ANY] * (5 + group),
        out_specs=(ANY,) * (2 + group),
        scratch_shapes=[
            pltpu.VMEM((count, 2, block, block), F32),
            pltpu.VMEM((slots, block, block), F32),
            pltpu.VMEM((slots, block, block), F32),
            pltpu.VMEM((slots, block, block), F32),
            half_type, half_type, half_type, half_type, half_type, half_type,
            pltpu.VMEM((2, block, block), BF16),
            pltpu.VMEM((2, block, block), BF16),
            half_type, half_type,
            pltpu.VMEM((block, block), F32),
            pltpu.VMEM((group, 2, rows, block), F32),
            pltpu.VMEM((group, 2, rows, block), F32),
            pltpu.VMEM((group, rows, block), F32),
            pltpu.SemaphoreType.DMA((4,)),
            pltpu.SemaphoreType.DMA((n, base)),
            pltpu.SemaphoreType.DMA((count, group)),
            pltpu.SemaphoreType.DMA((count, group)),
            pltpu.SemaphoreType.DMA((n * base,)),
            pltpu.SemaphoreType.DMA((1,)),
            pltpu.SemaphoreType.DMA((group,)),
            pltpu.SemaphoreType.DMA((group,)),
            pltpu.SemaphoreType.DMA((group,)),
            pltpu.SemaphoreType.DMA((group,)),
            pltpu.SemaphoreType.DMA((group,)),
        ],
        compiler_params=pltpu.CompilerParams(vmem_limit_bytes=VMEM_LIMIT, collective_id=0, has_side_effects=True),
        name="lanes",
    )(table, packed, left_basis, right_basis, second_moment, early, *arrived)

    def backward(caps):
        def run(backs, table, got, rank_moment, second_moment):
            arrived = exchange(caps, backs)
            update, moment_out = pl.pallas_call(
                functools.partial(settle_kernel, layout),
                out_shape=(
                    jax.ShapeDtypeStruct((rows, width), F32),
                    jax.ShapeDtypeStruct((slots, block, block), F32),
                ),
                in_specs=[SMEM, ANY, ANY, ANY],
                out_specs=(ANY, ANY),
                scratch_shapes=[
                    pltpu.VMEM((rows, width), F32),
                    pltpu.VMEM((slots, block, block), F32),
                    pltpu.SemaphoreType.DMA((col_blocks,)),
                    pltpu.SemaphoreType.DMA((slots,)),
                    pltpu.SemaphoreType.DMA((col_blocks + slots,)),
                ],
                compiler_params=pltpu.CompilerParams(vmem_limit_bytes=VMEM_LIMIT),
                cost_estimate=pl.CostEstimate(
                    flops=rows * width, bytes_accessed=8 * (rows * width + slots * block * block), transcendentals=0
                ),
                name="settle",
            )(table, got, rank_moment, second_moment)
            return arrived, update, moment_out
        return run

    arrived, update, moment_out = lax.switch(
        branch, [backward(caps) for caps in found], backs, table, got, rank_moment, second_moment
    )
    update = pl.pallas_call(
        functools.partial(close_kernel, layout, place_at),
        out_shape=jax.ShapeDtypeStruct((rows, width), F32),
        in_specs=[SMEM] + [ANY] * (group + 1),
        out_specs=ANY,
        scratch_shapes=[
            pltpu.VMEM((group, rows, block), F32),
            pltpu.SemaphoreType.DMA((group,)),
            pltpu.SemaphoreType.DMA((group,)),
        ],
        input_output_aliases={group + 1: 0},
        name="close",
    )(table, *arrived, update)
    return update, momentum_out, moment_out


def per_device(gradient, momentum, left_basis, right_basis, second_moment, block_slot):
    n = lax.axis_size("dp")
    n_mp = lax.axis_size("mp")
    rows, width = gradient.shape
    slots, block, _ = left_basis.shape
    col_blocks = width // block
    group = block // rows
    row_sets = block_slot.shape[0] // (col_blocks * n_mp)
    ranks = -(-col_blocks // n)
    count = ranks * row_sets
    me = lax.axis_index("dp")
    my_set = me // group

    base = ranks - 1
    paired = row_sets == 2 and n == 2 * group and n * (2 * ranks - 1) == 2 * col_blocks and base >= 2 and slots > 2 * base
    if paired and n_mp % 2 == 0:
        return paired_step(gradient, momentum, left_basis, right_basis, second_moment, block_slot, ranks, group)

    sets = jnp.arange(row_sets, dtype=jnp.int32)[:, None]
    grid = block_slot.reshape(n_mp, row_sets, col_blocks)[lax.axis_index("mp")]
    owner, local = grid // slots % n, grid % slots
    same = owner[:, :, None] == owner[:, None, :]
    lower = local[:, None, :] < local[:, :, None]
    rank = jnp.sum((same & lower).astype(jnp.int32), axis=-1)
    place = (owner * ranks + rank)[my_set]
    order = rank * row_sets + sets
    mine = (owner == me).reshape(-1)
    order, local = order.reshape(-1), local.reshape(-1)
    hit = mine[None, :] & (order[None, :] == jnp.arange(count, dtype=jnp.int32)[:, None])
    slot_of = jnp.sum(jnp.where(hit, local[None, :], 0), axis=1)
    held = mine[None, :] & (local[None, :] == jnp.arange(slots, dtype=jnp.int32)[:, None])
    rank_of = jnp.sum(jnp.where(held, order[None, :], 0), axis=1)
    live = jnp.sum(held.astype(jnp.int32), axis=1)

    cols = max(c for c in (1, 2, 3, 4, 6) if col_blocks % c == 0)
    packed, momentum_out = pl.pallas_call(
        functools.partial(pack_kernel, cols, block),
        out_shape=(
            jax.ShapeDtypeStruct((n * ranks, 2, rows, block), F32),
            jax.ShapeDtypeStruct((rows, width), F32),
        ),
        in_specs=[SMEM, ANY, ANY],
        out_specs=(ANY, ANY),
        scratch_shapes=[
            pltpu.VMEM((rows, width), F32),
            pltpu.VMEM((rows, width), F32),
            pltpu.VMEM((rows, width), F32),
            pltpu.SemaphoreType.DMA((col_blocks // cols, 2)),
            pltpu.SemaphoreType.DMA((col_blocks // cols, 2 * cols + 1)),
        ],
        compiler_params=pltpu.CompilerParams(vmem_limit_bytes=VMEM_LIMIT),
        name="pack",
    )(place, gradient, momentum)

    half_type = pltpu.VMEM((block, block), BF16)
    got, rank_moment = pl.pallas_call(
        functools.partial(step_kernel, n, ranks, row_sets, group),
        out_shape=(
            jax.ShapeDtypeStruct((n * ranks, rows, block), F32),
            jax.ShapeDtypeStruct((count, block, block), F32),
        ),
        in_specs=[SMEM, ANY, ANY, ANY, ANY],
        out_specs=(ANY, ANY),
        scratch_shapes=[
            pltpu.VMEM((count, 2, block, block), F32),
            pltpu.VMEM((slots, block, block), F32),
            pltpu.VMEM((slots, block, block), F32),
            pltpu.VMEM((slots, block, block), F32),
            half_type, half_type, half_type, half_type, half_type, half_type,
            pltpu.VMEM((2, block, block), BF16),
            pltpu.VMEM((2, block, block), BF16),
            half_type, half_type,
            pltpu.VMEM((2, block, block), F32),
            pltpu.SemaphoreType.DMA((3,)),
            pltpu.SemaphoreType.DMA((n, ranks)),
            pltpu.SemaphoreType.DMA((count, group)),
            pltpu.SemaphoreType.DMA((count, group)),
            pltpu.SemaphoreType.DMA((n * ranks,)),
            pltpu.SemaphoreType.DMA((2,)),
        ],
        compiler_params=pltpu.CompilerParams(
            vmem_limit_bytes=VMEM_LIMIT, collective_id=0, has_side_effects=True
        ),
        name="step",
    )(slot_of, packed, left_basis, right_basis, second_moment)

    update, moment_out = pl.pallas_call(
        functools.partial(place_kernel, block),
        out_shape=(
            jax.ShapeDtypeStruct((rows, width), F32),
            jax.ShapeDtypeStruct((slots, block, block), F32),
        ),
        in_specs=[SMEM, SMEM, SMEM, ANY, ANY, ANY],
        out_specs=(ANY, ANY),
        scratch_shapes=[
            pltpu.VMEM((rows, width), F32),
            pltpu.VMEM((slots, block, block), F32),
            pltpu.SemaphoreType.DMA((col_blocks,)),
            pltpu.SemaphoreType.DMA((slots,)),
            pltpu.SemaphoreType.DMA((col_blocks + slots,)),
        ],
        compiler_params=pltpu.CompilerParams(vmem_limit_bytes=VMEM_LIMIT),
        name="place",
    )(place, rank_of, live, got, rank_moment, second_moment)
    return update, momentum_out, moment_out


def solution(mesh):
    rows = P(("mp", "dp"), None)
    state = P(("mp", "dp"), None, None)
    return jax.shard_map(
        per_device,
        mesh=mesh,
        in_specs=(rows, rows, state, state, state, P()),
        out_specs=(rows, rows, state),
        check_vma=False,
    )
```
